512 devices in a mesh: segment: 8 (over x, core), frames: 64 (over y, z).
Axes of the slice: x: 4, y: 4, z: 16, core: 2. Of those that a mesh axis runs over, the one named last changes fastest.
Arguments:
- hidden: bfloat16 [8, 16384, 1536], P('segment', 'frames'), may hold values from -3 to 3
- features: bfloat16 [4096, 768], P('frames'), may hold values from -160 to 160, as said below
- kv_weight: bfloat16 [8, 768, 3072], P('segment', None, 'frames'), may hold values from -0.21875 to 0.21875
- mod_table: float32 [8, 32, 3, 1536], P('segment'), may hold values from -4 to 4
- timestep: int32 [8, 256], P('segment', 'frames'), may hold values from 0 to 31
- block_list: int32 [8, 256, 4], P('segment', 'frames'), may hold values from 0 to 63
- block_count: int32 [8, 256], P('segment', 'frames'), may hold values from 1 to 4, as said below
Outputs:
- handed: bfloat16 [8, 16384, 1536], P('segment', 'frames')
The draws below stay inside these ranges and needn't reach their ends.
Inputs may be any that keep to these rules, and one draw needn't show every extreme that they name: `features`: drawn as normal values, rows may carry common scales; within the bounds given. `block_list`: entry j of a block's list counts when j < the block's count; the others are ignored. `block_count`: the 4 frame blocks of one device have at most 10 live list entries together, and in every section some device has exactly 10.
All inputs are finite; a program needn't handle non-finite values.
Results may differ from the reference program's by a relative error of at most 0.0044.
The reference program's roundings to bfloat16 on the way (of `queries`, `key_values`, `weights` and `output`) count: a program that leaves them out, or rounds other values in their place, can miss the bound.
Values may be sent and summed in bfloat16 or wider, within the bound.
No kernel may reach another device: no remote copies, remote signals or barrier semaphores. Data moves between devices by JAX's collectives and lax.ppermute only.
A program may use at most 64 MiB of HBM per device.

```python
import jax
import jax.numpy as jnp
from jax import lax

HEADS = 12
HD = 128
DW = 1536
FW = 768
BLK = 64
SEL = 4
NT = 32
SEGMENTS = 8
TOKENS = 16384
QB_DEV = 4
QBLK = 256
FEATS = 4096
FBLK = 64


def draw_features(key, part):
    key_base = jax.random.fold_in(jax.random.fold_in(key, 11), 0)
    base = jax.random.normal(key_base, (FEATS, FW), jnp.float32)
    values = jnp.clip(base, -6.0, 6.0)
    return values.astype(jnp.bfloat16)


def draw_block_count(key, part):
    groups = QBLK // QB_DEV
    key_busy, key_forced, key_rank, key_light = jax.random.split(jax.random.fold_in(key, 23), 4)
    busy = jax.random.randint(key_busy, (SEGMENTS, groups), 0, 3) == 0
    forced = jax.random.randint(key_forced, (SEGMENTS, 1), 0, groups)
    busy = busy | (jnp.arange(groups, dtype=jnp.int32)[None, :] == forced)
    rank_keys = jax.random.randint(key_rank, (SEGMENTS, groups, QB_DEV), 0, 1 << 20) * QB_DEV + jnp.arange(QB_DEV, dtype=jnp.int32)
    ranks = jnp.argsort(jnp.argsort(rank_keys, axis=-1), axis=-1)
    heavy = jnp.where(ranks < QB_DEV // 2, SEL, 1)
    light = jax.random.randint(key_light, (SEGMENTS, groups, QB_DEV), 1, SEL // 2 + 1)
    counts = jnp.where(busy[:, :, None], heavy, light)
    return counts.reshape(SEGMENTS, QBLK).astype(jnp.int32)


def touch_ends(result, stream_key, least, top_value):
    longest = result.shape.index(max(result.shape))
    spots = []
    for shift in (0, 1):
        where = [jax.random.randint(jax.random.fold_in(stream_key, axis), (), 0, length) for axis, length in enumerate(result.shape)]
        where[longest] = (where[longest] + shift) % result.shape[longest]
        spots.append(tuple(where))
    return result.at[spots[0]].set(least).at[spots[1]].set(top_value)


def level_of(rng, dims, cuts, smallest, largest):
    gain, own = 1.0, jax.random.fold_in(rng, 6)
    for dim, shards_of in cuts:
        draws = jnp.exp(jax.random.uniform(jax.random.fold_in(own, dim), (shards_of,), jnp.float32, smallest / len(cuts), largest / len(cuts)))
        gain = gain * jnp.repeat(draws, dims[dim] // shards_of).reshape([-1 if axis == dim else 1 for axis in range(len(dims))])
    return gain


def centred(own_key, shape, scale, reach, cuts=(), held_as=jnp.bfloat16):
    gain = level_of(own_key, shape, cuts, -0.22, 0.18) if cuts else 1.0
    entries = jax.random.normal(own_key, shape, jnp.float32) * scale * gain
    return jnp.minimum(jnp.maximum(entries, -reach), reach).astype(held_as)


def setup_inputs(seed: int = 0) -> dict:
    key_of = jax.random.split(jax.random.key(seed), 8)
    return {
        "hidden": centred(key_of[0], (SEGMENTS, TOKENS, DW), 0.5, 3.0, ((0, 8), (1, 64))),
        "features": draw_features(jax.random.fold_in(key_of[7], 71), 0),
        "kv_weight": centred(key_of[2], (SEGMENTS, FW, 2 * DW), FW ** -0.5, 0.21875, ((0, 8), (2, 64))),
        "mod_table": centred(key_of[3], (SEGMENTS, NT, 3, DW), 1.5, 4.0, ((0, 8),), jnp.float32),
        "timestep": touch_ends(jax.random.randint(key_of[4], (SEGMENTS, QBLK), 0, NT), jax.random.fold_in(key_of[4], 1), 0, NT - 1).astype(jnp.int32),
        "block_list": touch_ends(jax.random.randint(key_of[5], (SEGMENTS, QBLK, SEL), 0, FBLK), jax.random.fold_in(key_of[5], 1), 0, FBLK - 1).astype(jnp.int32),
        "block_count": draw_block_count(jax.random.fold_in(key_of[7], 71), 0),
    }


def reference(hidden, features, kv_weight, mod_table, timestep, block_list, block_count):
    segment_outputs = []
    offsets = jnp.arange(BLK, dtype=jnp.int32)
    for segment_index in range(SEGMENTS):
        key_values = jnp.dot(features, kv_weight[segment_index], preferred_element_type=jnp.float32).astype(jnp.bfloat16)
        stream = hidden[segment_index].astype(jnp.float32)
        normed = stream * lax.rsqrt(lax.optimization_barrier(jnp.mean(stream * stream, axis=-1, keepdims=True)) + 1e-06)
        modulate = mod_table[segment_index][timestep[segment_index]]

        def attend_block(inputs):
            stream_block, normed_block, mod_block, list_blocks, list_count = inputs
            queries = (normed_block * (1.0 + mod_block[1]) + mod_block[0]).astype(jnp.bfloat16)
            query_heads = queries.reshape(BLK, HEADS, HD).astype(jnp.float32)
            row_index = (list_blocks[:, None] * BLK + offsets[None, :]).reshape(-1).astype(jnp.int32)
            gathered = key_values[row_index]
            key_heads = gathered[:, :DW].reshape(-1, HEADS, HD).astype(jnp.float32)
            value_heads = gathered[:, DW:].reshape(-1, HEADS, HD).astype(jnp.float32)
            scores = jnp.einsum('qhd,khd->hqk', query_heads, key_heads) * (1.0 / HD ** 0.5)
            key_mask = jnp.repeat(jnp.arange(SEL, dtype=jnp.int32) < list_count, BLK)
            scores = jnp.where(key_mask[None, None, :], scores, jnp.float32(-1e+30))
            top_score = lax.optimization_barrier(jnp.max(scores, axis=-1, keepdims=True))
            expo = jnp.exp(scores - top_score)
            weights = (expo / lax.optimization_barrier(jnp.sum(expo, axis=-1, keepdims=True))).astype(jnp.bfloat16)
            attended = jnp.einsum('hqk,khd->qhd', weights.astype(jnp.float32), value_heads).reshape(BLK, DW)
            return (stream_block + mod_block[2] * attended).astype(jnp.bfloat16)
        blocks_out = lax.map(attend_block, (stream.reshape(QBLK, BLK, DW), normed.reshape(QBLK, BLK, DW), modulate, block_list[segment_index], block_count[segment_index]))
        segment_outputs.append(blocks_out.reshape(TOKENS, DW))
    output = jnp.stack(segment_outputs)
    return jnp.roll(output, 1, axis=0)
```

```python
import jax
import jax.numpy as jnp
from jax import lax
from jax.experimental import pallas as pl
from jax.experimental.pallas import tpu as pltpu
from jax.sharding import PartitionSpec as P

HEADS = 12
HD = 128
BLK = 64
DW = 1536
FW = 768
SEL = 4
LIVE = 10
Y = 4
Z = 16
SEG = 8
PART = BLK // SEG
COLS = 48
HALF = DW // 2
Y_GROUPS = [[y * Z + z for y in range(Y)] for z in range(Z)]
Z_GROUPS = [[y * Z + z for z in range(Z)] for y in range(Y)]


def from_behind(block, axis, distance):
    devices = range(lax.axis_size(axis))
    route = [((i - distance) % len(devices), i) for i in devices]
    return lax.ppermute(block, axis, route)


def attend(first, start, count, x_ref, q_ref, hid_ref, gate_ref, w_ref, out_ref, wv, kv, sem):
    copies = []
    for i, part in enumerate((0, 2, 1, 3)):
        copy = pltpu.make_async_copy(w_ref.at[:, part], wv.at[part], sem.at[i])
        copy.start()
        copies.append(copy)
    inv_root = 1.0 / HD**0.5
    slot = lax.broadcasted_iota(jnp.int32, (BLK, SEL * BLK), 1) // BLK
    for half in range(2):
        for i, part in ((2 * half, half), (2 * half + 1, half + 2)):
            copies[i].wait()
            w = wv[part].reshape(Z * COLS, FW)
            kv[part] = lax.dot_general(
                x_ref[...], w, (((1,), (1,)), ((), ())), preferred_element_type=jnp.float32
            ).astype(jnp.bfloat16)
        for b in range(4):
            rows = slice(b * BLK, (b + 1) * BLK)
            window = pl.ds(pl.multiple_of(first[b] * BLK, BLK), SEL * BLK)
            here = slot + first[b]
            mask = (here >= start[b]) & (here < start[b] + count[b])
            for h in range(HEADS // 2):
                inner = slice(h * HD, (h + 1) * HD)
                cols = slice(half * HALF + h * HD, half * HALF + (h + 1) * HD)
                scores = lax.dot_general(
                    q_ref[rows, cols],
                    kv[half, window, inner],
                    (((1,), (1,)), ((), ())),
                    preferred_element_type=jnp.float32,
                )
                scores = jnp.where(mask, scores * inv_root, jnp.float32(-1e30))
                top = jnp.max(scores, axis=-1, keepdims=True)
                expo = jnp.exp(scores - top)
                weights = (expo / jnp.sum(expo, axis=-1, keepdims=True)).astype(jnp.bfloat16)
                mixed = jnp.dot(weights, kv[half + 2, window, inner], preferred_element_type=jnp.float32)
                out_ref[rows, cols] = (
                    hid_ref[rows, cols].astype(jnp.float32) + gate_ref[b : b + 1, cols] * mixed
                ).astype(jnp.bfloat16)


def attention(first, start, count, x, q, hidden, gate, w):
    whole = lambda: pl.BlockSpec(memory_space=pltpu.VMEM)
    return pl.pallas_call(
        attend,
        out_shape=jax.ShapeDtypeStruct((4 * BLK, DW), jnp.bfloat16),
        in_specs=[pl.BlockSpec(memory_space=pltpu.SMEM)] * 3
        + [whole(), whole(), whole(), whole(), pl.BlockSpec(memory_space=pltpu.HBM)],
        out_specs=whole(),
        scratch_shapes=[
            pltpu.VMEM((Y, Z, COLS, FW), jnp.bfloat16),
            pltpu.VMEM((Y, LIVE * BLK, HALF), jnp.bfloat16),
            pltpu.SemaphoreType.DMA((4,)),
        ],
        compiler_params=pltpu.CompilerParams(vmem_limit_bytes=40 * 1024 * 1024),
    )(first, start, count, x, q, hidden, gate, w)


def copy_rows(spot, table_ref, out_ref):
    for n in range(SEG * LIVE):
        out_ref[n] = table_ref[spot[n]]


def pick(spot, table):
    whole = pl.BlockSpec(memory_space=pltpu.VMEM)
    return pl.pallas_call(
        copy_rows,
        out_shape=jax.ShapeDtypeStruct((SEG * LIVE, PART, FW), jnp.bfloat16),
        in_specs=[pl.BlockSpec(memory_space=pltpu.SMEM), whole],
        out_specs=whole,
    )(spot, table)


def local(hidden, features, kv_weight, mod_table, timestep, block_list, block_count):
    slab = kv_weight[0].T
    slab = lax.all_gather(slab, "frames", axis=0, tiled=True, axis_index_groups=Y_GROUPS)
    features, slab, block_list = lax.optimization_barrier((features, slab, block_list))
    weight = lax.all_gather(slab, "frames", axis=0, tiled=True, axis_index_groups=Z_GROUPS)

    counts = block_count[0]
    before = jnp.arange(4, dtype=jnp.int32)[:, None] > jnp.arange(4, dtype=jnp.int32)[None, :]
    start = jnp.sum(jnp.where(before, counts[None, :], 0), axis=1)
    entry = jnp.arange(SEL, dtype=jnp.int32)[None, :]
    place = jnp.where(entry < counts[:, None], start[:, None] + entry, -1)
    hit = place[None] == jnp.arange(LIVE, dtype=jnp.int32)[:, None, None]
    wanted = jnp.sum(jnp.where(hit, block_list[0][None], 0), axis=(1, 2))
    wanted = lax.all_gather(wanted[None], "segment", axis=0, tiled=True)

    part = lax.dynamic_slice(features, (lax.axis_index("segment") * PART, 0), (PART, FW))
    table = lax.all_gather(part, "frames", axis=0, tiled=True, axis_index_groups=Y_GROUPS)
    table = lax.all_gather(table, "frames", axis=0, tiled=True, axis_index_groups=Z_GROUPS)
    table = table.reshape(Z * Y, PART, FW)
    spot = (wanted % Z) * Y + wanted // Z
    picked = pick(spot.reshape(-1), table)
    picked = lax.all_to_all(picked.reshape(SEG, LIVE * PART, FW), "segment", 0, 0)
    picked = picked.reshape(SEG, LIVE, PART, FW).transpose(1, 0, 2, 3).reshape(LIVE * BLK, FW)

    stream = hidden[0].astype(jnp.float32)
    normed = stream * lax.rsqrt(jnp.mean(stream * stream, axis=-1, keepdims=True) + 1e-06)
    levels = mod_table.shape[1]
    onehot = (timestep[0][:, None] == jnp.arange(levels, dtype=jnp.int32)[None, :]).astype(jnp.float32)
    modulate = jnp.sum(onehot[:, :, None, None] * mod_table[0][None], axis=1)
    queries = (
        normed.reshape(4, BLK, DW) * (1.0 + modulate[:, 1][:, None, :]) + modulate[:, 0][:, None, :]
    ).astype(jnp.bfloat16)

    first = jnp.minimum(start, LIVE - SEL)
    result = attention(
        first,
        start,
        counts,
        picked,
        queries.reshape(4 * BLK, DW),
        hidden[0],
        modulate[:, 2],
        weight.reshape(Z, Y, COLS, FW),
    )
    return from_behind(result[None], "segment", 1)


def solution(mesh):
    placed = (
        P("segment", "frames", None),
        P("frames", None),
        P("segment", None, "frames"),
        P("segment", None, None, None),
        P("segment", "frames"),
        P("segment", "frames", None),
        P("segment", "frames"),
    )
    return jax.shard_map(
        local, mesh=mesh, in_specs=placed, out_specs=P("segment", "frames", None), check_vma=False
    )
```

```python
import jax
import jax.numpy as jnp
from jax import lax
from jax.experimental import pallas as pl
from jax.experimental.pallas import tpu as pltpu
from jax.sharding import PartitionSpec as P

HEADS = 12
HD = 128
BLK = 64
DW = 1536
FW = 768
SEL = 4
LIVE = 10
Y = 4
Z = 16
SEG = 8
PART = BLK // SEG
COLS = 48
HALF = DW // 2
Y_GROUPS = [[y * Z + z for y in range(Y)] for z in range(Z)]
Z_GROUPS = [[y * Z + z for z in range(Z)] for y in range(Y)]


def from_behind(block, axis, distance):
    devices = range(lax.axis_size(axis))
    route = [((i - distance) % len(devices), i) for i in devices]
    return lax.ppermute(block, axis, route)


def attend(first, start, count, x_ref, q_ref, hid_ref, gate_ref, w_ref, out_ref, wv, kv, sem):
    copies = []
    for i, part in enumerate((0, 2, 1, 3)):
        copy = pltpu.make_async_copy(w_ref.at[:, part], wv.at[part], sem.at[i])
        copy.start()
        copies.append(copy)
    inv_root = 1.0 / HD**0.5
    slot = lax.broadcasted_iota(jnp.int32, (BLK, SEL * BLK), 1) // BLK
    windows = [pl.ds(pl.multiple_of(first[b] * BLK, BLK), SEL * BLK) for b in range(4)]

    def heads_of(half, b):
        rows = slice(b * BLK, (b + 1) * BLK)
        for h in range(HEADS // 2):
            cols = slice(half * HALF + h * HD, half * HALF + (h + 1) * HD)
            yield rows, cols, slice(h * HD, (h + 1) * HD)

    def scores_of(half, b):
        return [
            lax.dot_general(
                q_ref[rows, cols],
                kv[half, windows[b], inner],
                (((1,), (1,)), ((), ())),
                preferred_element_type=jnp.float32,
            )
            for rows, cols, inner in heads_of(half, b)
        ]

    for half in range(2):
        for i, part in ((2 * half, half), (2 * half + 1, half + 2)):
            copies[i].wait()
            kv[part] = lax.dot_general(
                x_ref[...],
                wv[part].reshape(Z * COLS, FW),
                (((1,), (1,)), ((), ())),
                preferred_element_type=jnp.float32,
            ).astype(jnp.bfloat16)
        ahead = scores_of(half, 0)
        for b in range(4):
            scores = ahead
            if b < 3:
                ahead = scores_of(half, b + 1)
            here = slot + first[b]
            mask = (here >= start[b]) & (here < start[b] + count[b])
            weights = []
            for score in scores:
                score = jnp.where(mask, score * inv_root, jnp.float32(-1e30))
                expo = jnp.exp(score - jnp.max(score, axis=-1, keepdims=True))
                weights.append((expo / jnp.sum(expo, axis=-1, keepdims=True)).astype(jnp.bfloat16))
            for weight, (rows, cols, inner) in zip(weights, heads_of(half, b)):
                mixed = jnp.dot(
                    weight, kv[half + 2, windows[b], inner], preferred_element_type=jnp.float32
                )
                out_ref[rows, cols] = (
                    hid_ref[rows, cols].astype(jnp.float32) + gate_ref[b : b + 1, cols] * mixed
                ).astype(jnp.bfloat16)


def attention(first, start, count, x, q, hidden, gate, w):
    whole = lambda: pl.BlockSpec(memory_space=pltpu.VMEM)
    return pl.pallas_call(
        attend,
        out_shape=jax.ShapeDtypeStruct((4 * BLK, DW), jnp.bfloat16),
        in_specs=[pl.BlockSpec(memory_space=pltpu.SMEM)] * 3
        + [whole(), whole(), whole(), whole(), pl.BlockSpec(memory_space=pltpu.HBM)],
        out_specs=whole(),
        scratch_shapes=[
            pltpu.VMEM((Y, Z, COLS, FW), jnp.bfloat16),
            pltpu.VMEM((Y, LIVE * BLK, HALF), jnp.bfloat16),
            pltpu.SemaphoreType.DMA((4,)),
        ],
        compiler_params=pltpu.CompilerParams(vmem_limit_bytes=40 * 1024 * 1024),
    )(first, start, count, x, q, hidden, gate, pltpu.with_memory_space_constraint(w, pltpu.HBM))


def copy_rows(spot, table_ref, out_ref):
    for n in range(SEG * LIVE):
        out_ref[n] = table_ref[spot[n]]


def pick(spot, table):
    whole = pl.BlockSpec(memory_space=pltpu.VMEM)
    return pl.pallas_call(
        copy_rows,
        out_shape=jax.ShapeDtypeStruct((SEG * LIVE, PART, FW), jnp.bfloat16),
        in_specs=[pl.BlockSpec(memory_space=pltpu.SMEM), whole],
        out_specs=whole,
    )(spot, table)


def local(hidden, features, kv_weight, mod_table, timestep, block_list, block_count):
    me = lax.axis_index("segment")
    slab = from_behind(kv_weight[0].T, "segment", 1)
    stream_in = from_behind(hidden[0], "segment", 1)
    levels = mod_table.shape[1]
    onehot = (timestep[0][:, None] == jnp.arange(levels, dtype=jnp.int32)[None, :]).astype(jnp.float32)
    modulate = jnp.sum(onehot[:, :, None, None] * mod_table[0][None], axis=1)
    modulate = from_behind(modulate.reshape(12, DW), "segment", 1).reshape(4, 3, DW)

    counts = block_count[0]
    before = jnp.arange(4, dtype=jnp.int32)[:, None] > jnp.arange(4, dtype=jnp.int32)[None, :]
    start = jnp.sum(jnp.where(before, counts[None, :], 0), axis=1)
    entry = jnp.arange(SEL, dtype=jnp.int32)[None, :]
    place = jnp.where(entry < counts[:, None], start[:, None] + entry, -1)
    hit = place[None] == jnp.arange(LIVE, dtype=jnp.int32)[:, None, None]
    wanted = jnp.sum(jnp.where(hit, block_list[0][None], 0), axis=(1, 2))
    lists = jnp.concatenate([wanted, start, counts]).reshape(1, LIVE + 8)
    lists = lax.all_gather(lists, "segment", axis=0, tiled=True)
    lists = jnp.roll(lists, 1, axis=0)
    spot = (lists[:, :LIVE] % Z) * Y + lists[:, :LIVE] // Z
    mine = lax.dynamic_slice(lists, (me, LIVE), (1, 8))[0]

    slab, spot = lax.optimization_barrier((slab, spot))
    slab = lax.all_gather(slab, "frames", axis=0, tiled=True, axis_index_groups=Y_GROUPS)
    features, slab = lax.optimization_barrier((features, slab))
    weight = lax.all_gather(slab, "frames", axis=0, tiled=True, axis_index_groups=Z_GROUPS)

    part = lax.dynamic_slice(features, (me * PART, 0), (PART, FW))
    table = lax.all_gather(part, "frames", axis=0, tiled=True, axis_index_groups=Y_GROUPS)
    table = lax.all_gather(table, "frames", axis=0, tiled=True, axis_index_groups=Z_GROUPS)
    picked = pick(spot.reshape(-1), table.reshape(Z * Y, PART, FW))
    picked = lax.all_to_all(picked.reshape(SEG, LIVE * PART, FW), "segment", 0, 0)
    picked = picked.reshape(SEG, LIVE, PART, FW).transpose(1, 0, 2, 3).reshape(LIVE * BLK, FW)

    stream = stream_in.astype(jnp.float32)
    normed = stream * lax.rsqrt(jnp.mean(stream * stream, axis=-1, keepdims=True) + 1e-06)
    queries = (
        normed.reshape(4, BLK, DW) * (1.0 + modulate[:, 1][:, None, :]) + modulate[:, 0][:, None, :]
    ).astype(jnp.bfloat16)

    result = attention(
        jnp.minimum(mine[:4], LIVE - SEL),
        mine[:4],
        mine[4:],
        picked,
        queries.reshape(4 * BLK, DW),
        stream_in,
        modulate[:, 2],
        weight.reshape(Z, Y, COLS, FW),
    )
    return result[None]


def solution(mesh):
    placed = (
        P("segment", "frames", None),
        P("frames", None),
        P("segment", None, "frames"),
        P("segment", None, None, None),
        P("segment", "frames"),
        P("segment", "frames", None),
        P("segment", "frames"),
    )
    return jax.shard_map(
        local, mesh=mesh, in_specs=placed, out_specs=P("segment", "frames", None), check_vma=False
    )
```

```python
import jax
import jax.numpy as jnp
from jax import lax
from jax.experimental import pallas as pl
from jax.experimental.pallas import tpu as pltpu
from jax.sharding import PartitionSpec as P

HEADS = 12
HD = 128
BLK = 64
DW = 1536
FW = 768
SEL = 4
LIVE = 10
Y = 4
Z = 16
SEG = 8
PART = BLK // SEG
COLS = 48
HALF = DW // 2
Y_GROUPS = [[y * Z + z for y in range(Y)] for z in range(Z)]
Z_GROUPS = [[y * Z + z for z in range(Z)] for y in range(Y)]


def from_behind(block, axis, distance):
    devices = range(lax.axis_size(axis))
    route = [((i - distance) % len(devices), i) for i in devices]
    return lax.ppermute(block, axis, route)


def attend(first, start, count, x_ref, q_ref, hid_ref, gate_ref, w_ref, out_ref, wv, kv, sem):
    copies = []
    for i, part in enumerate((0, 2, 1, 3)):
        copy = pltpu.make_async_copy(w_ref.at[:, part], wv.at[part], sem.at[i])
        copy.start()
        copies.append(copy)
    inv_root = 1.0 / HD**0.5
    slot = lax.broadcasted_iota(jnp.int32, (BLK, SEL * BLK), 1) // BLK
    windows = [pl.ds(pl.multiple_of(first[b] * BLK, BLK), SEL * BLK) for b in range(4)]

    def heads_of(half, b):
        rows = slice(b * BLK, (b + 1) * BLK)
        for h in range(HEADS // 2):
            cols = slice(half * HALF + h * HD, half * HALF + (h + 1) * HD)
            yield rows, cols, slice(h * HD, (h + 1) * HD)

    def scores_of(half, b):
        return [
            lax.dot_general(
                q_ref[rows, cols],
                kv[half, windows[b], inner],
                (((1,), (1,)), ((), ())),
                preferred_element_type=jnp.float32,
            )
            for rows, cols, inner in heads_of(half, b)
        ]

    for half in range(2):
        for i, part in ((2 * half, half), (2 * half + 1, half + 2)):
            copies[i].wait()
            kv[part] = lax.dot_general(
                x_ref[...],
                wv[part].reshape(Z * COLS, FW),
                (((1,), (1,)), ((), ())),
                preferred_element_type=jnp.float32,
            ).astype(jnp.bfloat16)
        ahead = scores_of(half, 0)
        for b in range(4):
            scores = ahead
            if b < 3:
                ahead = scores_of(half, b + 1)
            here = slot + first[b]
            mask = (here >= start[b]) & (here < start[b] + count[b])
            weights = []
            for score in scores:
                score = jnp.where(mask, score * inv_root, jnp.float32(-1e30))
                expo = jnp.exp(score - jnp.max(score, axis=-1, keepdims=True))
                weights.append((expo / jnp.sum(expo, axis=-1, keepdims=True)).astype(jnp.bfloat16))
            for weight, (rows, cols, inner) in zip(weights, heads_of(half, b)):
                mixed = jnp.dot(
                    weight, kv[half + 2, windows[b], inner], preferred_element_type=jnp.float32
                )
                out_ref[rows, cols] = (
                    hid_ref[rows, cols].astype(jnp.float32) + gate_ref[b : b + 1, cols] * mixed
                ).astype(jnp.bfloat16)


def attention(first, start, count, x, q, hidden, gate, w):
    whole = lambda: pl.BlockSpec(memory_space=pltpu.VMEM)
    return pl.pallas_call(
        attend,
        out_shape=jax.ShapeDtypeStruct((4 * BLK, DW), jnp.bfloat16),
        in_specs=[pl.BlockSpec(memory_space=pltpu.SMEM)] * 3
        + [whole(), whole(), whole(), whole(), pl.BlockSpec(memory_space=pltpu.HBM)],
        out_specs=whole(),
        scratch_shapes=[
            pltpu.VMEM((Y, Z, COLS, FW), jnp.bfloat16),
            pltpu.VMEM((Y, LIVE * BLK, HALF), jnp.bfloat16),
            pltpu.SemaphoreType.DMA((4,)),
        ],
        compiler_params=pltpu.CompilerParams(vmem_limit_bytes=40 * 1024 * 1024),
    )(first, start, count, x, q, hidden, gate, pltpu.with_memory_space_constraint(w, pltpu.HBM))


def copy_rows(spot, table_ref, out_ref):
    for n in range(SEG * LIVE):
        out_ref[n] = table_ref[spot[n]]


def pick(spot, table):
    whole = pl.BlockSpec(memory_space=pltpu.VMEM)
    return pl.pallas_call(
        copy_rows,
        out_shape=jax.ShapeDtypeStruct((SEG * LIVE, PART, FW), jnp.bfloat16),
        in_specs=[pl.BlockSpec(memory_space=pltpu.SMEM), whole],
        out_specs=whole,
    )(spot, table)


def local(hidden, features, kv_weight, mod_table, timestep, block_list, block_count):
    me = lax.axis_index("segment")
    slab = from_behind(kv_weight[0].T, "segment", 1)
    slab = lax.all_gather(slab, "frames", axis=0, tiled=True, axis_index_groups=Y_GROUPS)
    features, slab, block_count, mod_table, hidden = lax.optimization_barrier((features, slab, block_count, mod_table, hidden))
    weight = lax.all_gather(slab, "frames", axis=0, tiled=True, axis_index_groups=Z_GROUPS)
    stream_in = from_behind(hidden[0], "segment", 1)
    levels = mod_table.shape[1]
    onehot = (timestep[0][:, None] == jnp.arange(levels, dtype=jnp.int32)[None, :]).astype(jnp.float32)
    modulate = jnp.sum(onehot[:, :, None, None] * mod_table[0][None], axis=1)
    modulate = from_behind(modulate.reshape(12, DW), "segment", 1).reshape(4, 3, DW)

    counts = block_count[0]
    before = jnp.arange(4, dtype=jnp.int32)[:, None] > jnp.arange(4, dtype=jnp.int32)[None, :]
    start = jnp.sum(jnp.where(before, counts[None, :], 0), axis=1)
    entry = jnp.arange(SEL, dtype=jnp.int32)[None, :]
    place = jnp.where(entry < counts[:, None], start[:, None] + entry, -1)
    hit = place[None] == jnp.arange(LIVE, dtype=jnp.int32)[:, None, None]
    wanted = jnp.sum(jnp.where(hit, block_list[0][None], 0), axis=(1, 2))
    lists = jnp.concatenate([wanted, start, counts]).reshape(1, LIVE + 8)
    lists = lax.all_gather(lists, "segment", axis=0, tiled=True)
    lists = jnp.roll(lists, 1, axis=0)
    spot = lists[:, :LIVE]
    mine = lax.dynamic_slice(lists, (me, LIVE), (1, 8))[0]


    part = lax.dynamic_slice(features, (me * PART, 0), (PART, FW))
    table = lax.all_to_all(jnp.broadcast_to(part[None], (Z, PART, FW)), "frames", 0, 0, axis_index_groups=Z_GROUPS)
    table = lax.all_gather(table.reshape(Z * PART, FW), "frames", axis=0, tiled=True, axis_index_groups=Y_GROUPS)
    picked = pick(spot.reshape(-1), table.reshape(Z * Y, PART, FW))
    picked = lax.all_to_all(picked.reshape(SEG, LIVE * PART, FW), "segment", 0, 0)
    picked = picked.reshape(SEG, LIVE, PART, FW).transpose(1, 0, 2, 3).reshape(LIVE * BLK, FW)

    stream = stream_in.astype(jnp.float32)
    normed = stream * lax.rsqrt(jnp.mean(stream * stream, axis=-1, keepdims=True) + 1e-06)
    queries = (
        normed.reshape(4, BLK, DW) * (1.0 + modulate[:, 1][:, None, :]) + modulate[:, 0][:, None, :]
    ).astype(jnp.bfloat16)

    result = attention(
        jnp.minimum(mine[:4], LIVE - SEL),
        mine[:4],
        mine[4:],
        picked,
        queries.reshape(4 * BLK, DW),
        stream_in,
        modulate[:, 2],
        weight.reshape(Z, Y, COLS, FW),
    )
    return result[None]


def solution(mesh):
    placed = (
        P("segment", "frames", None),
        P("frames", None),
        P("segment", None, "frames"),
        P("segment", None, None, None),
        P("segment", "frames"),
        P("segment", "frames", None),
        P("segment", "frames"),
    )
    return jax.shard_map(
        local, mesh=mesh, in_specs=placed, out_specs=P("segment", "frames", None), check_vma=False
    )
```

```python
import jax
import jax.numpy as jnp
from jax import lax
from jax.experimental import pallas as pl
from jax.experimental.pallas import tpu as pltpu
from jax.sharding import PartitionSpec as P

HEADS = 12
HD = 128
BLK = 64
DW = 1536
FW = 768
SEL = 4
LIVE = 10
Y = 4
Z = 16
SEG = 8
PART = BLK // SEG
COLS = 48
HALF = DW // 2
Y_GROUPS = [[y * Z + z for y in range(Y)] for z in range(Z)]
Z_GROUPS = [[y * Z + z for z in range(Z)] for y in range(Y)]


def from_behind(block, axis, distance):
    devices = range(lax.axis_size(axis))
    route = [((i - distance) % len(devices), i) for i in devices]
    return lax.ppermute(block, axis, route)


def attend(first, start, count, x_ref, q_ref, hid_ref, gate_ref, w_ref, out_ref, wv, kv, sem):
    copies = []
    for i, part in enumerate((0, 2, 1, 3)):
        copy = pltpu.make_async_copy(w_ref.at[:, part], wv.at[i], sem.at[i])
        copy.start()
        copies.append(copy)
    inv_root = 1.0 / HD**0.5
    slot = lax.broadcasted_iota(jnp.int32, (BLK, SEL * BLK), 1) // BLK
    windows = [pl.ds(pl.multiple_of(first[b] * BLK, BLK), SEL * BLK) for b in range(4)]

    def heads_of(half, b):
        rows = slice(b * BLK, (b + 1) * BLK)
        for h in range(HEADS // 2):
            keys = 2 * half * HALF + h * HD
            cols = slice(half * HALF + h * HD, half * HALF + (h + 1) * HD)
            yield rows, cols, slice(keys, keys + HD), slice(keys + HALF, keys + HALF + HD)

    def scores_of(half, b):
        return [
            lax.dot_general(
                q_ref[rows, cols],
                kv[windows[b], keys],
                (((1,), (1,)), ((), ())),
                preferred_element_type=jnp.float32,
            )
            for rows, cols, keys, _ in heads_of(half, b)
        ]

    for half in range(2):
        for copy in copies[2 * half : 2 * half + 2]:
            copy.wait()
        kv[:, half * DW : (half + 1) * DW] = lax.dot_general(
            x_ref[...],
            wv[2 * half : 2 * half + 2].reshape(DW, FW),
            (((1,), (1,)), ((), ())),
            preferred_element_type=jnp.float32,
        ).astype(jnp.bfloat16)
        ahead = scores_of(half, 0)
        for b in range(4):
            scores = ahead
            if b < 3:
                ahead = scores_of(half, b + 1)
            here = slot + first[b]
            mask = (here >= start[b]) & (here < start[b] + count[b])
            weights = []
            for score in scores:
                score = jnp.where(mask, score * inv_root, jnp.float32(-1e30))
                expo = jnp.exp(score - jnp.max(score, axis=-1, keepdims=True))
                weights.append((expo / jnp.sum(expo, axis=-1, keepdims=True)).astype(jnp.bfloat16))
            for weight, (rows, cols, _, vals) in zip(weights, heads_of(half, b)):
                mixed = jnp.dot(weight, kv[windows[b], vals], preferred_element_type=jnp.float32)
                out_ref[rows, cols] = (
                    hid_ref[rows, cols].astype(jnp.float32) + gate_ref[b : b + 1, cols] * mixed
                ).astype(jnp.bfloat16)


def attention(first, start, count, x, q, hidden, gate, w):
    whole = lambda: pl.BlockSpec(memory_space=pltpu.VMEM)
    return pl.pallas_call(
        attend,
        out_shape=jax.ShapeDtypeStruct((4 * BLK, DW), jnp.bfloat16),
        in_specs=[pl.BlockSpec(memory_space=pltpu.SMEM)] * 3
        + [whole(), whole(), whole(), whole(), pl.BlockSpec(memory_space=pltpu.HBM)],
        out_specs=whole(),
        scratch_shapes=[
            pltpu.VMEM((Y, Z, COLS, FW), jnp.bfloat16),
            pltpu.VMEM((LIVE * BLK, 2 * DW), jnp.bfloat16),
            pltpu.SemaphoreType.DMA((4,)),
        ],
        compiler_params=pltpu.CompilerParams(vmem_limit_bytes=40 * 1024 * 1024),
    )(first, start, count, x, q, hidden, gate, pltpu.with_memory_space_constraint(w, pltpu.HBM))


def copy_rows(spot, table_ref, out_ref):
    for n in range(SEG * LIVE):
        out_ref[n] = table_ref[spot[n]]


def pick(spot, table):
    whole = pl.BlockSpec(memory_space=pltpu.VMEM)
    return pl.pallas_call(
        copy_rows,
        out_shape=jax.ShapeDtypeStruct((SEG * LIVE, PART, FW), jnp.bfloat16),
        in_specs=[pl.BlockSpec(memory_space=pltpu.SMEM), whole],
        out_specs=whole,
    )(spot, table)


def local(hidden, features, kv_weight, mod_table, timestep, block_list, block_count):
    me = lax.axis_index("segment")
    slab = from_behind(kv_weight[0].T, "segment", 1)
    slab = lax.all_to_all(
        jnp.broadcast_to(slab[None], (Y, COLS, FW)), "frames", 0, 0, axis_index_groups=Y_GROUPS
    ).reshape(Y * COLS, FW)
    slab, block_count, mod_table, hidden = lax.optimization_barrier((slab, block_count, mod_table, hidden))
    weight = lax.all_gather(slab, "frames", axis=0, tiled=True, axis_index_groups=Z_GROUPS)
    stream_in = from_behind(hidden[0], "segment", 1)
    levels = mod_table.shape[1]
    onehot = (timestep[0][:, None] == jnp.arange(levels, dtype=jnp.int32)[None, :]).astype(jnp.float32)
    modulate = jnp.sum(onehot[:, :, None, None] * mod_table[0][None], axis=1)
    modulate = from_behind(modulate.reshape(12, DW), "segment", 1).reshape(4, 3, DW)

    counts = block_count[0]
    before = jnp.arange(4, dtype=jnp.int32)[:, None] > jnp.arange(4, dtype=jnp.int32)[None, :]
    start = jnp.sum(jnp.where(before, counts[None, :], 0), axis=1)
    entry = jnp.arange(SEL, dtype=jnp.int32)[None, :]
    place = jnp.where(entry < counts[:, None], start[:, None] + entry, -1)
    hit = place[None] == jnp.arange(LIVE, dtype=jnp.int32)[:, None, None]
    wanted = jnp.sum(jnp.where(hit, block_list[0][None], 0), axis=(1, 2))
    lists = jnp.concatenate([wanted, start, counts]).reshape(1, LIVE + 8)
    lists = lax.all_gather(lists, "segment", axis=0, tiled=True)
    lists = jnp.roll(lists, 1, axis=0)
    spot = lists[:, :LIVE]
    mine = lax.dynamic_slice(lists, (me, LIVE), (1, 8))[0]


    part = lax.dynamic_slice(features, (me * PART, 0), (PART, FW))
    table = lax.all_to_all(jnp.broadcast_to(part[None], (Z, PART, FW)), "frames", 0, 0, axis_index_groups=Z_GROUPS)
    table = lax.all_gather(table.reshape(Z * PART, FW), "frames", axis=0, tiled=True, axis_index_groups=Y_GROUPS)
    picked = pick(spot.reshape(-1), table.reshape(Z * Y, PART, FW))
    picked = lax.all_to_all(picked.reshape(SEG, LIVE * PART, FW), "segment", 0, 0)
    picked = picked.reshape(SEG, LIVE, PART, FW).transpose(1, 0, 2, 3).reshape(LIVE * BLK, FW)

    stream = stream_in.astype(jnp.float32)
    normed = stream * lax.rsqrt(jnp.mean(stream * stream, axis=-1, keepdims=True) + 1e-06)
    queries = (
        normed.reshape(4, BLK, DW) * (1.0 + modulate[:, 1][:, None, :]) + modulate[:, 0][:, None, :]
    ).astype(jnp.bfloat16)

    result = attention(
        jnp.minimum(mine[:4], LIVE - SEL),
        mine[:4],
        mine[4:],
        picked,
        queries.reshape(4 * BLK, DW),
        stream_in,
        modulate[:, 2],
        weight.reshape(Z, Y, COLS, FW),
    )
    return result[None]


def solution(mesh):
    placed = (
        P("segment", "frames", None),
        P("frames", None),
        P("segment", None, "frames"),
        P("segment", None, None, None),
        P("segment", "frames"),
        P("segment", "frames", None),
        P("segment", "frames"),
    )
    return jax.shard_map(
        local, mesh=mesh, in_specs=placed, out_specs=P("segment", "frames", None), check_vma=False
    )
```

```python
import jax
import jax.numpy as jnp
from jax import lax
from jax.experimental import pallas as pl
from jax.experimental.pallas import tpu as pltpu
from jax.sharding import PartitionSpec as P

HEADS = 12
HD = 128
BLK = 64
DW = 1536
FW = 768
SEL = 4
LIVE = 10
Y = 4
Z = 16
SEG = 8
PART = BLK // SEG
COLS = 48
HALF = DW // 2
Y_GROUPS = [[y * Z + z for y in range(Y)] for z in range(Z)]
Z_GROUPS = [[y * Z + z for z in range(Z)] for y in range(Y)]


def from_behind(block, axis, distance):
    devices = range(lax.axis_size(axis))
    route = [((i - distance) % len(devices), i) for i in devices]
    return lax.ppermute(block, axis, route)


def attend(first, start, count, x_ref, q_ref, hid_ref, gate_ref, w_ref, out_ref, wv, kv, held, sem, out_sem):
    copies = []
    for i, part in enumerate((0, 2, 1, 3)):
        copy = pltpu.make_async_copy(w_ref.at[:, part], wv.at[i], sem.at[i])
        copy.start()
        copies.append(copy)
    inv_root = 1.0 / HD**0.5
    slot = lax.broadcasted_iota(jnp.int32, (BLK, SEL * BLK), 1) // BLK
    windows = [pl.ds(pl.multiple_of(first[b] * BLK, BLK), SEL * BLK) for b in range(4)]

    def heads_of(half, b):
        rows = slice(b * BLK, (b + 1) * BLK)
        for h in range(HEADS // 2):
            keys = 2 * half * HALF + h * HD
            cols = slice(half * HALF + h * HD, half * HALF + (h + 1) * HD)
            yield rows, cols, slice(keys, keys + HD), slice(keys + HALF, keys + HALF + HD)

    def scores_of(half, b):
        return [
            lax.dot_general(
                q_ref[rows, cols],
                kv[windows[b], keys],
                (((1,), (1,)), ((), ())),
                preferred_element_type=jnp.float32,
            )
            for rows, cols, keys, _ in heads_of(half, b)
        ]

    sent = []
    for half in range(2):
        for copy in copies[2 * half : 2 * half + 2]:
            copy.wait()
        kv[:, half * DW : (half + 1) * DW] = lax.dot_general(
            x_ref[...],
            wv[2 * half : 2 * half + 2].reshape(DW, FW),
            (((1,), (1,)), ((), ())),
            preferred_element_type=jnp.float32,
        ).astype(jnp.bfloat16)
        ahead = scores_of(half, 0)
        for b in range(4):
            scores = ahead
            if b < 3:
                ahead = scores_of(half, b + 1)
            here = slot + first[b]
            mask = (here >= start[b]) & (here < start[b] + count[b])
            weights = []
            for score in scores:
                score = jnp.where(mask, score * inv_root, jnp.float32(-1e30))
                expo = jnp.exp(score - jnp.max(score, axis=-1, keepdims=True))
                weights.append((expo / jnp.sum(expo, axis=-1, keepdims=True)).astype(jnp.bfloat16))
            for weight, (rows, cols, _, vals) in zip(weights, heads_of(half, b)):
                mixed = jnp.dot(weight, kv[windows[b], vals], preferred_element_type=jnp.float32)
                held[rows, cols] = (
                    hid_ref[rows, cols].astype(jnp.float32) + gate_ref[b : b + 1, cols] * mixed
                ).astype(jnp.bfloat16)
            if half == 1:
                done = slice(b * BLK, (b + 1) * BLK)
                copy = pltpu.make_async_copy(held.at[done], out_ref.at[done], out_sem.at[b])
                copy.start()
                sent.append(copy)
    for copy in sent:
        copy.wait()


def attention(first, start, count, x, q, hidden, gate, w):
    whole = lambda: pl.BlockSpec(memory_space=pltpu.VMEM)
    return pl.pallas_call(
        attend,
        out_shape=jax.ShapeDtypeStruct((4 * BLK, DW), jnp.bfloat16),
        in_specs=[pl.BlockSpec(memory_space=pltpu.SMEM)] * 3
        + [whole(), whole(), whole(), whole(), pl.BlockSpec(memory_space=pltpu.HBM)],
        out_specs=pl.BlockSpec(memory_space=pltpu.HBM),
        scratch_shapes=[
            pltpu.VMEM((Y, Z, COLS, FW), jnp.bfloat16),
            pltpu.VMEM((LIVE * BLK, 2 * DW), jnp.bfloat16),
            pltpu.VMEM((4 * BLK, DW), jnp.bfloat16),
            pltpu.SemaphoreType.DMA((4,)),
            pltpu.SemaphoreType.DMA((4,)),
        ],
        compiler_params=pltpu.CompilerParams(vmem_limit_bytes=40 * 1024 * 1024),
    )(first, start, count, x, q, hidden, gate, pltpu.with_memory_space_constraint(w, pltpu.HBM))


def copy_rows(spot, table_ref, out_ref):
    for n in range(SEG * LIVE):
        out_ref[n] = table_ref[spot[n]]


def pick(spot, table):
    whole = pl.BlockSpec(memory_space=pltpu.VMEM)
    return pl.pallas_call(
        copy_rows,
        out_shape=jax.ShapeDtypeStruct((SEG * LIVE, PART, FW), jnp.bfloat16),
        in_specs=[pl.BlockSpec(memory_space=pltpu.SMEM), whole],
        out_specs=whole,
    )(spot, table)


def local(hidden, features, kv_weight, mod_table, timestep, block_list, block_count):
    me = lax.axis_index("segment")
    slab = from_behind(kv_weight[0].T, "segment", 1)
    slab = lax.all_to_all(
        jnp.broadcast_to(slab[None], (Y, COLS, FW)), "frames", 0, 0, axis_index_groups=Y_GROUPS
    ).reshape(Y * COLS, FW)
    slab, block_count, mod_table, hidden = lax.optimization_barrier((slab, block_count, mod_table, hidden))
    weight = lax.all_gather(slab, "frames", axis=0, tiled=True, axis_index_groups=Z_GROUPS)
    stream_in = from_behind(hidden[0], "segment", 1)
    levels = mod_table.shape[1]
    onehot = (timestep[0][:, None] == jnp.arange(levels, dtype=jnp.int32)[None, :]).astype(jnp.float32)
    modulate = jnp.sum(onehot[:, :, None, None] * mod_table[0][None], axis=1)
    modulate = from_behind(modulate.reshape(12, DW), "segment", 1).reshape(4, 3, DW)

    counts = block_count[0]
    before = jnp.arange(4, dtype=jnp.int32)[:, None] > jnp.arange(4, dtype=jnp.int32)[None, :]
    start = jnp.sum(jnp.where(before, counts[None, :], 0), axis=1)
    entry = jnp.arange(SEL, dtype=jnp.int32)[None, :]
    place = jnp.where(entry < counts[:, None], start[:, None] + entry, -1)
    hit = place[None] == jnp.arange(LIVE, dtype=jnp.int32)[:, None, None]
    wanted = jnp.sum(jnp.where(hit, block_list[0][None], 0), axis=(1, 2))
    lists = jnp.concatenate([wanted, start, counts]).reshape(1, LIVE + 8)
    lists = lax.all_gather(lists, "segment", axis=0, tiled=True)
    lists = jnp.roll(lists, 1, axis=0)
    spot = lists[:, :LIVE]
    mine = lax.dynamic_slice(lists, (me, LIVE), (1, 8))[0]


    part = lax.dynamic_slice(features, (me * PART, 0), (PART, FW))
    table = lax.all_to_all(jnp.broadcast_to(part[None], (Z, PART, FW)), "frames", 0, 0, axis_index_groups=Z_GROUPS)
    table = lax.all_gather(table.reshape(Z * PART, FW), "frames", axis=0, tiled=True, axis_index_groups=Y_GROUPS)
    picked = pick(spot.reshape(-1), table.reshape(Z * Y, PART, FW))
    picked = lax.all_to_all(picked.reshape(SEG, LIVE * PART, FW), "segment", 0, 0)
    picked = picked.reshape(SEG, LIVE, PART, FW).transpose(1, 0, 2, 3).reshape(LIVE * BLK, FW)

    stream = stream_in.astype(jnp.float32)
    normed = stream * lax.rsqrt(jnp.mean(stream * stream, axis=-1, keepdims=True) + 1e-06)
    queries = (
        normed.reshape(4, BLK, DW) * (1.0 + modulate[:, 1][:, None, :]) + modulate[:, 0][:, None, :]
    ).astype(jnp.bfloat16)

    result = attention(
        jnp.minimum(mine[:4], LIVE - SEL),
        mine[:4],
        mine[4:],
        picked,
        queries.reshape(4 * BLK, DW),
        stream_in,
        modulate[:, 2],
        weight.reshape(Z, Y, COLS, FW),
    )
    return result[None]


def solution(mesh):
    placed = (
        P("segment", "frames", None),
        P("frames", None),
        P("segment", None, "frames"),
        P("segment", None, None, None),
        P("segment", "frames"),
        P("segment", "frames", None),
        P("segment", "frames"),
    )
    return jax.shard_map(
        local, mesh=mesh, in_specs=placed, out_specs=P("segment", "frames", None), check_vma=False
    )
```

```python
import jax
import jax.numpy as jnp
from jax import lax
from jax.experimental import pallas as pl
from jax.experimental.pallas import tpu as pltpu
from jax.sharding import PartitionSpec as P

HEADS = 12
HD = 128
BLK = 64
DW = 1536
FW = 768
SEL = 4
LIVE = 10
Y = 4
Z = 16
SEG = 8
PART = BLK // SEG
COLS = 48
HALF = DW // 2
Y_GROUPS = [[y * Z + z for y in range(Y)] for z in range(Z)]
Z_GROUPS = [[y * Z + z for z in range(Z)] for y in range(Y)]


def from_behind(block, axis, distance):
    devices = range(lax.axis_size(axis))
    route = [((i - distance) % len(devices), i) for i in devices]
    return lax.ppermute(block, axis, route)


def attend(first, start, count, x_ref, q_ref, hid_ref, gate_ref, w_ref, out_ref, wv, kv, held, sem, out_sem):
    copies = []
    for i, part in enumerate((0, 2, 1, 3)):
        copy = pltpu.make_async_copy(w_ref.at[:, part], wv.at[i], sem.at[i])
        copy.start()
        copies.append(copy)
    inv_root = 1.0 / HD**0.5
    slot = lax.broadcasted_iota(jnp.int32, (BLK, SEL * BLK), 1) // BLK
    windows = [pl.ds(pl.multiple_of(first[b] * BLK, BLK), SEL * BLK) for b in range(4)]

    def heads_of(half, b):
        rows = slice(b * BLK, (b + 1) * BLK)
        for h in range(HEADS // 2):
            keys = 2 * half * HALF + h * HD
            cols = slice(half * HALF + h * HD, half * HALF + (h + 1) * HD)
            yield rows, cols, slice(keys, keys + HD), slice(keys + HALF, keys + HALF + HD)

    def scores_of(half, b):
        return [
            lax.dot_general(
                q_ref[rows, cols],
                kv[windows[b], keys],
                (((1,), (1,)), ((), ())),
                preferred_element_type=jnp.float32,
            )
            for rows, cols, keys, _ in heads_of(half, b)
        ]

    sent = []
    for half in range(2):
        for copy in copies[2 * half : 2 * half + 2]:
            copy.wait()
        kv[:, half * DW : (half + 1) * DW] = lax.dot_general(
            x_ref[...],
            wv[2 * half : 2 * half + 2].reshape(DW, FW),
            (((1,), (1,)), ((), ())),
            preferred_element_type=jnp.float32,
        ).astype(jnp.bfloat16)
        ahead = scores_of(half, 0)
        for b in range(4):
            scores = ahead
            if b < 3:
                ahead = scores_of(half, b + 1)
            here = slot + first[b]
            mask = (here >= start[b]) & (here < start[b] + count[b])
            weights = []
            for score in scores:
                score = jnp.where(mask, score * inv_root, jnp.float32(-1e30))
                expo = jnp.exp(score - jnp.max(score, axis=-1, keepdims=True))
                weights.append((expo / jnp.sum(expo, axis=-1, keepdims=True)).astype(jnp.bfloat16))
            for weight, (rows, cols, _, vals) in zip(weights, heads_of(half, b)):
                mixed = jnp.dot(weight, kv[windows[b], vals], preferred_element_type=jnp.float32)
                held[rows, cols] = (
                    hid_ref[rows, cols].astype(jnp.float32) + gate_ref[b : b + 1, cols] * mixed
                ).astype(jnp.bfloat16)
            if half == 1:
                done = slice(b * BLK, (b + 1) * BLK)
                copy = pltpu.make_async_copy(held.at[done], out_ref.at[done], out_sem.at[b])
                copy.start()
                sent.append(copy)
    for copy in sent:
        copy.wait()


def attention(first, start, count, x, q, hidden, gate, w):
    whole = lambda: pl.BlockSpec(memory_space=pltpu.VMEM)
    return pl.pallas_call(
        attend,
        out_shape=jax.ShapeDtypeStruct((4 * BLK, DW), jnp.bfloat16),
        in_specs=[pl.BlockSpec(memory_space=pltpu.SMEM)] * 3
        + [whole(), whole(), whole(), whole(), pl.BlockSpec(memory_space=pltpu.HBM)],
        out_specs=pl.BlockSpec(memory_space=pltpu.HBM),
        scratch_shapes=[
            pltpu.VMEM((Y, Z, COLS, FW), jnp.bfloat16),
            pltpu.VMEM((LIVE * BLK, 2 * DW), jnp.bfloat16),
            pltpu.VMEM((4 * BLK, DW), jnp.bfloat16),
            pltpu.SemaphoreType.DMA((4,)),
            pltpu.SemaphoreType.DMA((4,)),
        ],
        compiler_params=pltpu.CompilerParams(vmem_limit_bytes=40 * 1024 * 1024),
    )(first, start, count, x, q, hidden, gate, pltpu.with_memory_space_constraint(w, pltpu.HBM))


def copy_rows(spot, table_ref, out_ref):
    for n in range(SEG * LIVE):
        out_ref[n] = table_ref[spot[n]]


def pick(spot, table):
    whole = pl.BlockSpec(memory_space=pltpu.VMEM)
    return pl.pallas_call(
        copy_rows,
        out_shape=jax.ShapeDtypeStruct((SEG * LIVE, PART, FW), jnp.bfloat16),
        in_specs=[pl.BlockSpec(memory_space=pltpu.SMEM), whole],
        out_specs=whole,
    )(spot, table)


def local(hidden, features, kv_weight, mod_table, timestep, block_list, block_count):
    me = lax.axis_index("segment")
    slab = from_behind(kv_weight[0].T, "segment", 1)
    slab = lax.all_to_all(
        jnp.broadcast_to(slab[None], (Y, COLS, FW)), "frames", 0, 0, axis_index_groups=Y_GROUPS
    ).reshape(Y * COLS, FW)
    slab, block_count, mod_table, hidden = lax.optimization_barrier((slab, block_count, mod_table, hidden))
    weight = lax.all_gather(slab, "frames", axis=0, tiled=True, axis_index_groups=Z_GROUPS)
    counts = block_count[0]
    before = jnp.arange(4, dtype=jnp.int32)[:, None] > jnp.arange(4, dtype=jnp.int32)[None, :]
    start = jnp.sum(jnp.where(before, counts[None, :], 0), axis=1)
    entry = jnp.arange(SEL, dtype=jnp.int32)[None, :]
    place = jnp.where(entry < counts[:, None], start[:, None] + entry, -1)
    hit = place[None] == jnp.arange(LIVE, dtype=jnp.int32)[:, None, None]
    wanted = jnp.sum(jnp.where(hit, block_list[0][None], 0), axis=(1, 2))
    lists = jnp.concatenate([wanted, start, counts]).reshape(1, LIVE + 8)
    lists = lax.all_gather(lists, "segment", axis=0, tiled=True)
    lists = jnp.roll(lists, 1, axis=0)
    spot = lists[:, :LIVE]
    mine = lax.dynamic_slice(lists, (me, LIVE), (1, 8))[0]


    part = lax.dynamic_slice(features, (me * PART, 0), (PART, FW))
    table = lax.all_to_all(jnp.broadcast_to(part[None], (Z, PART, FW)), "frames", 0, 0, axis_index_groups=Z_GROUPS)
    table = lax.all_gather(table.reshape(Z * PART, FW), "frames", axis=0, tiled=True, axis_index_groups=Y_GROUPS)
    table, mod_table, hidden = lax.optimization_barrier((table, mod_table, hidden))
    stream_in = from_behind(hidden[0], "segment", 1)
    levels = mod_table.shape[1]
    onehot = (timestep[0][:, None] == jnp.arange(levels, dtype=jnp.int32)[None, :]).astype(jnp.float32)
    modulate = jnp.sum(onehot[:, :, None, None] * mod_table[0][None], axis=1)
    modulate = from_behind(modulate.reshape(12, DW), "segment", 1).reshape(4, 3, DW)

    picked = pick(spot.reshape(-1), table.reshape(Z * Y, PART, FW))
    picked = lax.all_to_all(picked.reshape(SEG, LIVE * PART, FW), "segment", 0, 0)
    picked = picked.reshape(SEG, LIVE, PART, FW).transpose(1, 0, 2, 3).reshape(LIVE * BLK, FW)

    stream = stream_in.astype(jnp.float32)
    normed = stream * lax.rsqrt(jnp.mean(stream * stream, axis=-1, keepdims=True) + 1e-06)
    queries = (
        normed.reshape(4, BLK, DW) * (1.0 + modulate[:, 1][:, None, :]) + modulate[:, 0][:, None, :]
    ).astype(jnp.bfloat16)

    result = attention(
        jnp.minimum(mine[:4], LIVE - SEL),
        mine[:4],
        mine[4:],
        picked,
        queries.reshape(4 * BLK, DW),
        stream_in,
        modulate[:, 2],
        weight.reshape(Z, Y, COLS, FW),
    )
    return result[None]


def solution(mesh):
    placed = (
        P("segment", "frames", None),
        P("frames", None),
        P("segment", None, "frames"),
        P("segment", None, None, None),
        P("segment", "frames"),
        P("segment", "frames", None),
        P("segment", "frames"),
    )
    return jax.shard_map(
        local, mesh=mesh, in_specs=placed, out_specs=P("segment", "frames", None), check_vma=False
    )
```
